32 devices in a mesh: gx: 4 (over z), gy: 4 (over x, core), gz: 2 (over y).
Axes of the slice: x: 2, y: 2, z: 4, core: 2. Of those that a mesh axis runs over, the one named last changes fastest.
Arguments:
- density: float32 [3, 64, 256, 256], P(None, 'gx', 'gy', 'gz'), may hold values from -6 to 6
- efficiency: float32 [64, 256, 256], P('gx', 'gy', 'gz'), may hold values from 0.5 to 2
Outputs:
- ionized: float32 [3, 64, 256, 256], P(None, 'gx', 'gy', 'gz')
The draws below stay inside these ranges and needn't reach their ends.
All inputs are finite; a program needn't handle non-finite values.
Results may differ from the reference program's by a relative error of at most 0.00005.
Values sent between devices are 32-bit elements; how exact they have to be, the bound alone decides.
A program may use at most 128 MiB of HBM per device.

```python
import math
import jax
import jax.numpy as jnp

SNAPS = 3
R_SMALL = 4
R_LARGE = 8
NX = 64
NY = 256
NZ = 256


def levels(key, shape, cuts, smallest, top_value):
    gain = 1.0
    for axis_at, blocks in cuts:
        steps = jax.random.uniform(jax.random.fold_in(jax.random.fold_in(key, 6), axis_at), (blocks,), jnp.float32, smallest / len(cuts), top_value / len(cuts))
        gain = gain * jnp.repeat(jnp.exp(steps), shape[axis_at] // blocks).reshape((-1,) + (1,) * (len(shape) - 1 - axis_at))
    return gain


def gaussian(own_key, dims, width, bound, split=(), kind=jnp.bfloat16):
    factor_of = levels(own_key, dims, split, -0.22, 0.18) if split else 1.0
    values = jax.random.normal(own_key, dims, jnp.float32) * width * factor_of
    return jnp.minimum(jnp.maximum(values, -bound), bound).astype(kind)


def setup_inputs(seed: int = 0) -> dict:
    splits = jax.random.split(jax.random.key(seed), 3)
    return {
        "density": gaussian(splits[0], (SNAPS, NX, NY, NZ), 1.0, 6.0, ((1, 4), (2, 4), (3, 2)), jnp.float32),
        "efficiency": jnp.clip(jnp.exp(math.log(2.0) - 1.3862944 * jax.random.uniform(splits[1], (NX, NY, NZ), jnp.float32) ** levels(splits[1], (NX, NY, NZ), ((0, 4), (1, 4), (2, 2)), -0.2, 0.2)), 0.5, 2.0),
    }


def profile(radius):
    offsets = jnp.arange(-radius, radius + 1).astype(jnp.float32)
    raw_weights = 1.0 - (offsets / (radius + 1.0)) ** 2
    return raw_weights / jnp.sqrt(jnp.sum(raw_weights * raw_weights))

def smooth(volume, radius):
    weights = profile(radius)
    for axis_dim in (3, 2, 1):
        total = jnp.zeros_like(volume)
        for index in range(2 * radius + 1):
            total = total + weights[index] * jnp.roll(volume, radius - index, axis_dim)
        volume = total
    return volume

def reference(density, efficiency):
    smooth_small = smooth(density, R_SMALL)
    smooth_large = smooth(density, R_LARGE)
    level_small = efficiency[None] * smooth_small - 0.3
    level_large = efficiency[None] * smooth_large - 0.1
    return jnp.clip(0.5 + 0.25 * jnp.maximum(level_small, level_large), 0.0, 1.0)
```

```python
import functools
import math

import jax
import jax.numpy as jnp
from jax import lax
from jax.experimental import pallas as pl
from jax.experimental.pallas import tpu as pltpu
from jax.sharding import PartitionSpec as P

R_SMALL = 4
R_LARGE = 8
RADII = (R_SMALL, R_LARGE)
H = R_LARGE
GROUP = 16
F32 = jnp.float32
BF16 = jnp.bfloat16
MESH = pl.DeviceIdType.MESH


def scale_of(radius):
    raw = [(radius + 1) ** 2 - k * k for k in range(-radius, radius + 1)]
    return 1.0 / math.sqrt(sum(value * value for value in raw)) ** 3


def band(offset, radius):
    value = (radius + 1) ** 2 - offset * offset
    return jnp.where(jnp.abs(offset) <= radius, value, 0).astype(F32).astype(BF16)


def split(value):
    high = value.astype(BF16)
    return high, (value - high.astype(F32)).astype(BF16)


def iota(shape, dim):
    return lax.broadcasted_iota(jnp.int32, shape, dim)


def kernel(dens, eff, out, ext, effv, xb, zb, zm, zsend, zrecv, wy, wm, wh, outv,
           x_send, x_recv, y_send, y_recv, f_send, f_recv, z_send, z_recv,
           own_sem, eff_sem, out_sem):
    snaps, nx, ny, nz = dens.shape
    rows = ny + 2 * H
    groups = rows // GROUP
    near = {}
    for axis in ("gx", "gy", "gz"):
        count = lax.axis_size(axis)
        me = lax.axis_index(axis)
        near[axis] = (lax.rem(me + 1, count), lax.rem(me + count - 1, count))

    def own_copy(s):
        return pltpu.make_async_copy(
            dens.at[s], ext.at[s, pl.ds(H, nx), pl.ds(H, ny)], own_sem.at[s])

    eff_copy = pltpu.make_async_copy(eff, effv, eff_sem)

    def out_copy(s):
        return pltpu.make_async_copy(outv.at[s], out.at[s], out_sem.at[s])

    def group_rows(g):
        if g == 0:
            return 0, H
        if g == groups - 1:
            return ny - H, H
        return g * GROUP - H, GROUP

    def x_copy(s, g, d):
        start, size = group_rows(g)
        source = nx - H if d == 0 else 0
        target = 0 if d == 0 else nx + H
        return pltpu.make_async_remote_copy(
            src_ref=dens.at[s, pl.ds(source, H), pl.ds(start, size)],
            dst_ref=ext.at[s, pl.ds(target, H), pl.ds(H + start, size)],
            send_sem=x_send.at[s, g, d], recv_sem=x_recv.at[s, g, d],
            device_id={"gx": near["gx"][d]}, device_id_type=MESH)

    def y_copy(s, d):
        source = ny - H if d == 0 else 0
        target = 0 if d == 0 else ny + H
        return pltpu.make_async_remote_copy(
            src_ref=dens.at[s, :, pl.ds(source, H)],
            dst_ref=ext.at[s, pl.ds(H, nx), pl.ds(target, H)],
            send_sem=y_send.at[s, d], recv_sem=y_recv.at[s, d],
            device_id={"gy": near["gy"][d]}, device_id_type=MESH)

    def f_copy(s, q, d):
        planes = 0 if q == 0 else nx + H
        source = ny if d == 0 else H
        target = 0 if d == 0 else ny + H
        return pltpu.make_async_remote_copy(
            src_ref=ext.at[s, pl.ds(planes, H), pl.ds(source, H)],
            dst_ref=ext.at[s, pl.ds(planes, H), pl.ds(target, H)],
            send_sem=f_send.at[s, q, d], recv_sem=f_recv.at[s, q, d],
            device_id={"gy": near["gy"][d]}, device_id_type=MESH)

    def z_copy(s, d):
        return pltpu.make_async_remote_copy(
            src_ref=zsend.at[s, d], dst_ref=zrecv.at[s, d],
            send_sem=z_send.at[s, d], recv_sem=z_recv.at[s, d],
            device_id={"gz": near["gz"][d]}, device_id_type=MESH)

    for s in range(snaps):
        own_copy(s).start()
    eff_copy.start()

    barrier = pltpu.get_barrier_semaphore()
    for axis in ("gx", "gy", "gz"):
        for d in range(2):
            pl.semaphore_signal(
                barrier, inc=1, device_id={axis: near[axis][d]}, device_id_type=MESH)
    pl.semaphore_wait(barrier, 6)

    edge = (0, groups - 1)
    inner = tuple(range(1, groups - 1))
    for s in range(snaps):
        for g in edge:
            for d in range(2):
                x_copy(s, g, d).start()
    for s in range(snaps):
        for d in range(2):
            y_copy(s, d).start()
    for s in range(snaps):
        for g in inner:
            for d in range(2):
                x_copy(s, g, d).start()

    for f, radius in enumerate(RADII):
        shape = (ny, rows)
        along = band(iota(shape, 1) - iota(shape, 0) - H, radius)
        wy[f] = jnp.concatenate([along, along], axis=1)
        shape = (nz, nz)
        along = band(iota(shape, 1) - iota(shape, 0), radius)
        wm[f] = jnp.concatenate([along, along], axis=0)
        shape = (nx * H, nz)
        slot = lax.div(iota(shape, 0), H)
        cell = lax.rem(iota(shape, 0), H)
        lane = iota(shape, 1)
        low = band(cell - H - lane, radius)
        high = band(cell + nz - lane, radius)
        zero = jnp.zeros_like(low)
        for p in range(nx):
            low_p = jnp.where(slot == p, low, zero)
            high_p = jnp.where(slot == (p + 1) % nx, high, zero)
            wh[f, p // 2, pl.ds(0, nx * H), pl.ds((p % 2) * nz, nz)] = low_p
            wh[f, p // 2, pl.ds(nx * H, nx * H), pl.ds((p % 2) * nz, nz)] = high_p

    for s in range(snaps):
        for d, g in ((0, groups - 1), (1, 0)):
            for q in range(2):
                x_copy(s, g, q).wait_recv()
                f_copy(s, q, d).start()

    def smooth_x(s, g):
        base = g * GROUP

        def one(i, carry):
            def plane(k):
                return ext[s, i + (H + k), pl.ds(base, GROUP)]

            center = plane(0)
            sums = [center * float((radius + 1) ** 2) for radius in RADII]
            for k in range(1, R_LARGE + 1):
                pair = plane(-k) + plane(k)
                for f, radius in enumerate(RADII):
                    if k <= radius:
                        sums[f] = sums[f] + pair * float((radius + 1) ** 2 - k * k)
            for f in range(2):
                high, low = split(sums[f])
                xb[f, i, pl.ds(base, GROUP)] = high
                xb[f, i, pl.ds(rows + base, GROUP)] = low
            return carry

        lax.fori_loop(0, nx, one, 0, unroll=4)

    slots = lax.div(iota((ny, nz), 1), H)

    def smooth_y(s):
        for f in range(2):
            up = jnp.zeros((ny, nz), F32)
            down = jnp.zeros((ny, nz), F32)
            for p in range(0, nx, 2):
                both = jnp.concatenate([xb[f, p], xb[f, p + 1]], axis=1)
                done = jnp.dot(wy[f], both, preferred_element_type=F32)
                for j in range(2):
                    value = done[:, j * nz:(j + 1) * nz]
                    rolled = pltpu.roll(value, ((p + j + 1) * H) % nz, 1)
                    up = jnp.where(slots == p + j, rolled, up)
                    down = jnp.where(slots == (p + j + 1) % nx, rolled, down)
                    high, low = split(value)
                    zb[f, p + j, :, pl.ds(0, nz)] = high
                    zb[f, p + j, :, pl.ds(nz, nz)] = low
            zsend[s, 0, pl.ds(f * ny, ny)] = up
            zsend[s, 1, pl.ds(f * ny, ny)] = down
        for d in range(2):
            z_copy(s, d).start()

    def main_z(s):
        slot = s % 2
        for f in range(2):
            for p in range(0, nx, 4):
                block = zb[f, pl.ds(p, 4)].reshape(4 * ny, 2 * nz)
                done = jnp.dot(block, wm[f], preferred_element_type=F32)
                zm[slot, f, pl.ds(p, 4)] = done.reshape(4, ny, nz)

    def finish(s):
        slot = s % 2
        for d in range(2):
            z_copy(s, d).wait_recv()
        halves = []
        for f in range(2):
            packed = jnp.concatenate(
                [zrecv[s, 0, pl.ds(f * ny, ny)], zrecv[s, 1, pl.ds(f * ny, ny)]], axis=1)
            halves.append(jnp.concatenate(split(packed), axis=0))
        for p in range(0, nx, 2):
            level = [None, None]
            for f, (radius, less) in enumerate(zip(RADII, (0.3, 0.1))):
                done = jnp.dot(halves[f], wh[f, p // 2], preferred_element_type=F32)
                done = done[:ny] + done[ny:]
                pair = []
                for j in range(2):
                    smooth = (zm[slot, f, p + j] + done[:, j * nz:(j + 1) * nz]) * scale_of(radius)
                    pair.append(effv[p + j] * smooth - less)
                level[f] = pair
            for j in range(2):
                outv[s, p + j] = jnp.maximum(level[0][j], level[1][j])
        out_copy(s).start()

    for s in range(snaps):
        own_copy(s).wait()
        for d in range(2):
            y_copy(s, d).wait_recv()
            for q in range(2):
                f_copy(s, q, d).wait_recv()
        for g in edge:
            smooth_x(s, g)
        for g in inner:
            for d in range(2):
                x_copy(s, g, d).wait_recv()
            smooth_x(s, g)
        smooth_y(s)
        main_z(s)
        if s == 0:
            eff_copy.wait()
        else:
            finish(s - 1)
    finish(snaps - 1)

    for s in range(snaps):
        for d in range(2):
            for g in range(groups):
                x_copy(s, g, d).wait_send()
            y_copy(s, d).wait_send()
            z_copy(s, d).wait_send()
            for q in range(2):
                f_copy(s, q, d).wait_send()
        out_copy(s).wait()


def on_device(density, efficiency):
    snaps, nx, ny, nz = density.shape
    rows = ny + 2 * H
    groups = rows // GROUP
    dma = pltpu.SemaphoreType.DMA
    level = pl.pallas_call(
        kernel,
        out_shape=jax.ShapeDtypeStruct(density.shape, F32),
        in_specs=[pl.BlockSpec(memory_space=pl.ANY)] * 2,
        out_specs=pl.BlockSpec(memory_space=pl.ANY),
        scratch_shapes=[
            pltpu.VMEM((snaps, nx + 2 * H, rows, nz), F32),
            pltpu.VMEM((nx, ny, nz), F32),
            pltpu.VMEM((2, nx, 2 * rows, nz), BF16),
            pltpu.VMEM((2, nx, ny, 2 * nz), BF16),
            pltpu.VMEM((2, 2, nx, ny, nz), F32),
            pltpu.VMEM((snaps, 2, 2 * ny, nx * H), F32),
            pltpu.VMEM((snaps, 2, 2 * ny, nx * H), F32),
            pltpu.VMEM((2, ny, 2 * rows), BF16),
            pltpu.VMEM((2, 2 * nz, nz), BF16),
            pltpu.VMEM((2, nx // 2, 2 * nx * H, 2 * nz), BF16),
            pltpu.VMEM((snaps, nx, ny, nz), F32),
            dma((snaps, groups, 2)), dma((snaps, groups, 2)),
            dma((snaps, 2)), dma((snaps, 2)),
            dma((snaps, 2, 2)), dma((snaps, 2, 2)),
            dma((snaps, 2)), dma((snaps, 2)),
            dma((snaps,)), dma, dma((snaps,)),
        ],
        compiler_params=pltpu.CompilerParams(
            collective_id=0, has_side_effects=True),
    )(density, efficiency)
    return jnp.clip(0.5 + 0.25 * level, 0.0, 1.0)


def solution(mesh):
    placed = (P(None, "gx", "gy", "gz"), P("gx", "gy", "gz"))
    return jax.shard_map(
        on_device, mesh=mesh, in_specs=placed, out_specs=P(None, "gx", "gy", "gz"), check_vma=False
    )
```

```python
import functools
import math

import jax
import jax.numpy as jnp
from jax import lax
from jax.experimental import pallas as pl
from jax.experimental.pallas import tpu as pltpu
from jax.sharding import PartitionSpec as P

R_SMALL = 4
R_LARGE = 8
RADII = (R_SMALL, R_LARGE)
H = R_LARGE
GROUP = 16
STRIP = 32
F32 = jnp.float32
BF16 = jnp.bfloat16
MESH = pl.DeviceIdType.MESH


def scale_of(radius):
    raw = [(radius + 1) ** 2 - k * k for k in range(-radius, radius + 1)]
    return 1.0 / math.sqrt(sum(value * value for value in raw)) ** 3


def band(offset, radius):
    value = (radius + 1) ** 2 - offset * offset
    return jnp.where(jnp.abs(offset) <= radius, value, 0).astype(F32).astype(BF16)


def split(value):
    high = value.astype(BF16)
    return high, (value - high.astype(F32)).astype(BF16)


def iota(shape, dim):
    return lax.broadcasted_iota(jnp.int32, shape, dim)


def kernel(dens, eff, outv, ext, effv, xb, zb, zm, zsend, zrecv, wy, wm, wh,
           x_send, x_recv, y_send, y_recv, f_send, f_recv, z_send, z_recv,
           own_sem, eff_sem, out_sem):
    out = None
    snaps, nx, ny, nz = dens.shape
    rows = ny + 2 * H
    groups = rows // GROUP
    strips = ny // STRIP
    wide = STRIP + 2 * H
    near = {}
    for axis in ("gx", "gy", "gz"):
        count = lax.axis_size(axis)
        me = lax.axis_index(axis)
        near[axis] = (lax.rem(me + 1, count), lax.rem(me + count - 1, count))

    def own_copy(s):
        return pltpu.make_async_copy(
            dens.at[s], ext.at[s, pl.ds(H, nx), pl.ds(H, ny)], own_sem.at[s])

    eff_copy = pltpu.make_async_copy(eff, effv, eff_sem)

    def out_copy(u):
        s, h = divmod(u, strips)
        part = pl.ds(h * STRIP, STRIP)
        return pltpu.make_async_copy(outv.at[s, :, part], out.at[s, :, part], out_sem.at[u])

    def group_rows(g):
        if g == 0:
            return 0, H
        if g == groups - 1:
            return ny - H, H
        return g * GROUP - H, GROUP

    def x_copy(s, g, d):
        start, size = group_rows(g)
        source = nx - H if d == 0 else 0
        target = 0 if d == 0 else nx + H
        return pltpu.make_async_remote_copy(
            src_ref=dens.at[s, pl.ds(source, H), pl.ds(start, size)],
            dst_ref=ext.at[s, pl.ds(target, H), pl.ds(H + start, size)],
            send_sem=x_send.at[s, g, d], recv_sem=x_recv.at[s, g, d],
            device_id={"gx": near["gx"][d]}, device_id_type=MESH)

    def y_copy(s, d):
        source = ny - H if d == 0 else 0
        target = 0 if d == 0 else ny + H
        return pltpu.make_async_remote_copy(
            src_ref=dens.at[s, :, pl.ds(source, H)],
            dst_ref=ext.at[s, pl.ds(H, nx), pl.ds(target, H)],
            send_sem=y_send.at[s, d], recv_sem=y_recv.at[s, d],
            device_id={"gy": near["gy"][d]}, device_id_type=MESH)

    def f_copy(s, q, d):
        planes = 0 if q == 0 else nx + H
        source = ny if d == 0 else H
        target = 0 if d == 0 else ny + H
        return pltpu.make_async_remote_copy(
            src_ref=ext.at[s, pl.ds(planes, H), pl.ds(source, H)],
            dst_ref=ext.at[s, pl.ds(planes, H), pl.ds(target, H)],
            send_sem=f_send.at[s, q, d], recv_sem=f_recv.at[s, q, d],
            device_id={"gy": near["gy"][d]}, device_id_type=MESH)

    def z_copy(u, d):
        return pltpu.make_async_remote_copy(
            src_ref=zsend.at[u, d], dst_ref=zrecv.at[u, d],
            send_sem=z_send.at[u, d], recv_sem=z_recv.at[u, d],
            device_id={"gz": near["gz"][d]}, device_id_type=MESH)

    for s in range(snaps):
        own_copy(s).start()
    eff_copy.start()

    barrier = pltpu.get_barrier_semaphore()
    for axis in ("gx", "gy", "gz"):
        for d in range(2):
            pl.semaphore_signal(
                barrier, inc=1, device_id={axis: near[axis][d]}, device_id_type=MESH)
    pl.semaphore_wait(barrier, 6)

    edge = (0, groups - 1)
    inner = tuple(range(1, groups - 1))
    for s in range(snaps):
        for g in edge:
            for d in range(2):
                x_copy(s, g, d).start()
    for s in range(snaps):
        for d in range(2):
            y_copy(s, d).start()
    for s in range(snaps):
        for g in inner:
            for d in range(2):
                x_copy(s, g, d).start()

    for f, radius in enumerate(RADII):
        shape = (STRIP, wide)
        along = band(iota(shape, 1) - iota(shape, 0) - H, radius)
        wy[f] = jnp.concatenate([along, along], axis=1)
        shape = (nz, nz)
        along = band(iota(shape, 1) - iota(shape, 0), radius)
        wm[f] = jnp.concatenate([along, along], axis=0)
        shape = (nx * H, nz)
        slot = lax.div(iota(shape, 0), H)
        cell = lax.rem(iota(shape, 0), H)
        lane = iota(shape, 1)
        low = band(cell - H - lane, radius)
        high = band(cell + nz - lane, radius)
        zero = jnp.zeros_like(low)
        for p in range(nx):
            low_p = jnp.where(slot == p, low, zero)
            high_p = jnp.where(slot == (p + 1) % nx, high, zero)
            wh[f, p // 2, pl.ds(0, nx * H), pl.ds((p % 2) * nz, nz)] = low_p
            wh[f, p // 2, pl.ds(nx * H, nx * H), pl.ds((p % 2) * nz, nz)] = high_p

    for s in range(snaps):
        for d, g in ((0, groups - 1), (1, 0)):
            for q in range(2):
                x_copy(s, g, q).wait_recv()
                f_copy(s, q, d).start()

    def smooth_x(s, g):
        base = g * GROUP

        def one(i, carry):
            def plane(k):
                return ext[s, i + (H + k), pl.ds(base, GROUP)]

            center = plane(0)
            sums = [center * float((radius + 1) ** 2) for radius in RADII]
            for k in range(1, R_LARGE + 1):
                pair = plane(-k) + plane(k)
                for f, radius in enumerate(RADII):
                    if k <= radius:
                        sums[f] = sums[f] + pair * float((radius + 1) ** 2 - k * k)
            for f in range(2):
                high, low = split(sums[f])
                xb[f, i, pl.ds(base, GROUP)] = high
                xb[f, i, pl.ds(rows + base, GROUP)] = low
            return carry

        lax.fori_loop(0, nx, one, 0, unroll=4)

    slots = lax.div(iota((STRIP, nz), 1), H)

    def smooth_y(u):
        base = (u % strips) * STRIP
        for f in range(2):
            up = jnp.zeros((STRIP, nz), F32)
            down = jnp.zeros((STRIP, nz), F32)
            for p in range(0, nx, 2):
                both = jnp.concatenate(
                    [jnp.concatenate([xb[f, p + j, pl.ds(base, wide)],
                                      xb[f, p + j, pl.ds(rows + base, wide)]], axis=0)
                     for j in range(2)], axis=1)
                done = jnp.dot(wy[f], both, preferred_element_type=F32)
                for j in range(2):
                    value = done[:, j * nz:(j + 1) * nz]
                    rolled = pltpu.roll(value, ((p + j + 1) * H) % nz, 1)
                    up = jnp.where(slots == p + j, rolled, up)
                    down = jnp.where(slots == (p + j + 1) % nx, rolled, down)
                    high, low = split(value)
                    zb[f, p + j, :, pl.ds(0, nz)] = high
                    zb[f, p + j, :, pl.ds(nz, nz)] = low
            zsend[u, 0, pl.ds(f * STRIP, STRIP)] = up
            zsend[u, 1, pl.ds(f * STRIP, STRIP)] = down
        for d in range(2):
            z_copy(u, d).start()

    def main_z(u):
        slot = u % 2
        for f in range(2):
            for p in range(0, nx, 8):
                block = zb[f, pl.ds(p, 8)].reshape(8 * STRIP, 2 * nz)
                done = jnp.dot(block, wm[f], preferred_element_type=F32)
                zm[slot, f, pl.ds(p, 8)] = done.reshape(8, STRIP, nz)

    def finish(u):
        slot = u % 2
        s, h = divmod(u, strips)
        part = pl.ds(h * STRIP, STRIP)
        for d in range(2):
            z_copy(u, d).wait_recv()
        halves = []
        for f in range(2):
            own = pl.ds(f * STRIP, STRIP)
            packed = jnp.concatenate([zrecv[u, 0, own], zrecv[u, 1, own]], axis=1)
            halves.append(jnp.concatenate(split(packed), axis=0))
        for p in range(0, nx, 2):
            level = []
            for f, (radius, less) in enumerate(zip(RADII, (0.3, 0.1))):
                done = jnp.dot(halves[f], wh[f, p // 2], preferred_element_type=F32)
                done = done[:STRIP] + done[STRIP:]
                pair = []
                for j in range(2):
                    smooth = (zm[slot, f, p + j] + done[:, j * nz:(j + 1) * nz]) * scale_of(radius)
                    pair.append(effv[p + j, part] * smooth - less)
                level.append(pair)
            for j in range(2):
                top = jnp.maximum(level[0][j], level[1][j])
                outv[s, p + j, part] = jnp.clip(0.5 + 0.25 * top, 0.0, 1.0)
        if out is not None:
            out_copy(u).start()

    units = snaps * strips
    for s in range(snaps):
        own_copy(s).wait()
        for d in range(2):
            y_copy(s, d).wait_recv()
            for q in range(2):
                f_copy(s, q, d).wait_recv()
        for g in edge:
            smooth_x(s, g)
        ready = 1
        for h in range(strips):
            last = min(((h + 1) * STRIP + 2 * H) // GROUP, groups - 1)
            for g in range(ready, last):
                for d in range(2):
                    x_copy(s, g, d).wait_recv()
                smooth_x(s, g)
            ready = max(ready, last)
            u = s * strips + h
            smooth_y(u)
            main_z(u)
            if u == 0:
                eff_copy.wait()
            else:
                finish(u - 1)
    finish(units - 1)

    for s in range(snaps):
        for d in range(2):
            for g in range(groups):
                x_copy(s, g, d).wait_send()
            y_copy(s, d).wait_send()
            for q in range(2):
                f_copy(s, q, d).wait_send()
    for u in range(units):
        for d in range(2):
            z_copy(u, d).wait_send()
        if out is not None:
            out_copy(u).wait()


def on_device(density, efficiency):
    snaps, nx, ny, nz = density.shape
    rows = ny + 2 * H
    groups = rows // GROUP
    units = snaps * (ny // STRIP)
    dma = pltpu.SemaphoreType.DMA
    return pl.pallas_call(
        kernel,
        out_shape=pltpu.VMEM(density.shape, F32),
        in_specs=[pl.BlockSpec(memory_space=pl.ANY)] * 2,
        out_specs=pl.BlockSpec(memory_space=pltpu.VMEM),
        scratch_shapes=[
            pltpu.VMEM((snaps, nx + 2 * H, rows, nz), F32),
            pltpu.VMEM((nx, ny, nz), F32),
            pltpu.VMEM((2, nx, 2 * rows, nz), BF16),
            pltpu.VMEM((2, nx, STRIP, 2 * nz), BF16),
            pltpu.VMEM((2, 2, nx, STRIP, nz), F32),
            pltpu.VMEM((units, 2, 2 * STRIP, nx * H), F32),
            pltpu.VMEM((units, 2, 2 * STRIP, nx * H), F32),
            pltpu.VMEM((2, STRIP, 2 * (STRIP + 2 * H)), BF16),
            pltpu.VMEM((2, 2 * nz, nz), BF16),
            pltpu.VMEM((2, nx // 2, 2 * nx * H, 2 * nz), BF16),
            dma((snaps, groups, 2)), dma((snaps, groups, 2)),
            dma((snaps, 2)), dma((snaps, 2)),
            dma((snaps, 2, 2)), dma((snaps, 2, 2)),
            dma((units, 2)), dma((units, 2)),
            dma((snaps,)), dma, dma((units,)),
        ],
        compiler_params=pltpu.CompilerParams(
            collective_id=0, has_side_effects=True),
    )(density, efficiency)


def solution(mesh):
    placed = (P(None, "gx", "gy", "gz"), P("gx", "gy", "gz"))
    return jax.shard_map(
        on_device, mesh=mesh, in_specs=placed, out_specs=P(None, "gx", "gy", "gz"), check_vma=False
    )
```

```python
import functools
import math

import jax
import jax.numpy as jnp
from jax import lax
from jax.experimental import pallas as pl
from jax.experimental.pallas import tpu as pltpu
from jax.sharding import PartitionSpec as P

R_SMALL = 4
R_LARGE = 8
RADII = (R_SMALL, R_LARGE)
H = R_LARGE
GROUP = 16
STRIP = 32
F32 = jnp.float32
BF16 = jnp.bfloat16
MESH = pl.DeviceIdType.MESH


def scale_of(radius):
    raw = [(radius + 1) ** 2 - k * k for k in range(-radius, radius + 1)]
    return 1.0 / math.sqrt(sum(value * value for value in raw)) ** 3


def band(offset, radius):
    value = (radius + 1) ** 2 - offset * offset
    return jnp.where(jnp.abs(offset) <= radius, value, 0).astype(F32).astype(BF16)


def split(value):
    high = value.astype(BF16)
    return high, (value - high.astype(F32)).astype(BF16)


def iota(shape, dim):
    return lax.broadcasted_iota(jnp.int32, shape, dim)


def kernel(dens, eff, outv, ext, effv, xb, zb, zm, zsend, zrecv, wy, wm, wh, near_x, tsend, trecv,
           x_send, x_recv, y_send, y_recv, f_send, f_recv, z_send, z_recv, t_send, t_recv,
           own_sem, eff_sem):
    snaps, nx, ny, nz = dens.shape
    rows = ny + 2 * H
    groups = rows // GROUP
    strips = ny // STRIP
    wide = STRIP + 2 * H
    near = {}
    for axis in ("gx", "gy", "gz"):
        count = lax.axis_size(axis)
        me = lax.axis_index(axis)
        near[axis] = (lax.rem(me + 1, count), lax.rem(me + count - 1, count))

    def own_copy(s):
        return pltpu.make_async_copy(
            dens.at[s], ext.at[s, pl.ds(H, nx), pl.ds(H, ny)], own_sem.at[s])

    eff_copy = pltpu.make_async_copy(eff, effv, eff_sem)

    final = snaps - 1
    edge = (0, groups - 1)
    inner = tuple(range(1, groups - 1))
    last = inner[-1]
    first_needed = (strips - 1) * STRIP // GROUP
    ordered = tuple(sorted(inner, key=lambda g: (g == last, g < first_needed)))

    def arrivals(s):
        return tuple((g,) for g in ordered) if s == final else (inner,)

    def x_copy(s, together, d):
        start = max(together[0] * GROUP - H, 0)
        size = min((together[-1] + 1) * GROUP - H, ny) - start
        source = nx - H if d == 0 else 0
        target = 0 if d == 0 else nx + H
        g = together[0]
        return pltpu.make_async_remote_copy(
            src_ref=dens.at[s, pl.ds(source, H), pl.ds(start, size)],
            dst_ref=ext.at[s, pl.ds(target, H), pl.ds(H + start, size)],
            send_sem=x_send.at[s, g, d], recv_sem=x_recv.at[s, g, d],
            device_id={"gx": near["gx"][d]}, device_id_type=MESH)

    def t_copy(d):
        return pltpu.make_async_remote_copy(
            src_ref=tsend.at[d], dst_ref=trecv.at[d],
            send_sem=t_send.at[d], recv_sem=t_recv.at[d],
            device_id={"gx": near["gx"][d]}, device_id_type=MESH)

    def y_copy(s, d):
        source = ny - H if d == 0 else 0
        target = 0 if d == 0 else ny + H
        return pltpu.make_async_remote_copy(
            src_ref=dens.at[s, :, pl.ds(source, H)],
            dst_ref=ext.at[s, pl.ds(H, nx), pl.ds(target, H)],
            send_sem=y_send.at[s, d], recv_sem=y_recv.at[s, d],
            device_id={"gy": near["gy"][d]}, device_id_type=MESH)

    def f_copy(s, q, d):
        planes = 0 if q == 0 else nx + H
        source = ny if d == 0 else H
        target = 0 if d == 0 else ny + H
        return pltpu.make_async_remote_copy(
            src_ref=ext.at[s, pl.ds(planes, H), pl.ds(source, H)],
            dst_ref=ext.at[s, pl.ds(planes, H), pl.ds(target, H)],
            send_sem=f_send.at[s, q, d], recv_sem=f_recv.at[s, q, d],
            device_id={"gy": near["gy"][d]}, device_id_type=MESH)

    def z_copy(u, d):
        return pltpu.make_async_remote_copy(
            src_ref=zsend.at[u, d], dst_ref=zrecv.at[u, d],
            send_sem=z_send.at[u, d], recv_sem=z_recv.at[u, d],
            device_id={"gz": near["gz"][d]}, device_id_type=MESH)

    for s in range(snaps):
        own_copy(s).start()
    eff_copy.start()

    barrier = pltpu.get_barrier_semaphore()
    for axis in ("gx", "gy", "gz"):
        for d in range(2):
            pl.semaphore_signal(
                barrier, inc=1, device_id={axis: near[axis][d]}, device_id_type=MESH)
    pl.semaphore_wait(barrier, 6)

    for s in range(snaps):
        for g in edge:
            for d in range(2):
                x_copy(s, (g,), d).start()
    for s in range(snaps):
        for d in range(2):
            y_copy(s, d).start()

    own_copy(final).wait()
    last_rows = pl.ds(last * GROUP, GROUP)
    pieces = lax.div(iota((GROUP, nz), 1), 2 * H)
    for d in range(2):
        packed = jnp.zeros((GROUP, nz), F32)
        for p in range(H):
            plane = ext[final, (nx if d == 0 else H) + p, last_rows]
            packed = jnp.where(pieces == p, pltpu.roll(plane, p * 2 * H + H, 1), packed)
        tsend[d] = packed
        t_copy(d).start()

    for s in range(snaps):
        for together in arrivals(s):
            for d in range(2):
                x_copy(s, together, d).start()

    for f, radius in enumerate(RADII):
        shape = (STRIP, wide)
        along = band(iota(shape, 1) - iota(shape, 0) - H, radius)
        wy[f] = jnp.concatenate([along, along], axis=1)
        shape = (nz, nz)
        along = band(iota(shape, 1) - iota(shape, 0), radius)
        wm[f] = jnp.concatenate([along, along], axis=0)
        shape = (nx * H, nz)
        slot = lax.div(iota(shape, 0), H)
        cell = lax.rem(iota(shape, 0), H)
        lane = iota(shape, 1)
        low = band(cell - H - lane, radius)
        high = band(cell + nz - lane, radius)
        zero = jnp.zeros_like(low)
        for p in range(nx):
            low_p = jnp.where(slot == p, low, zero)
            high_p = jnp.where(slot == (p + 1) % nx, high, zero)
            wh[f, p // 2, pl.ds(0, nx * H), pl.ds((p % 2) * nz, nz)] = low_p
            wh[f, p // 2, pl.ds(nx * H, nx * H), pl.ds((p % 2) * nz, nz)] = high_p

    for s in range(snaps):
        for d, g in ((0, groups - 1), (1, 0)):
            for q in range(2):
                x_copy(s, (g,), q).wait_recv()
                f_copy(s, q, d).start()

    def smooth_x(field, start, g):
        base = g * GROUP

        def one(i, carry):
            def plane(k):
                return field[i + (H + k), pl.ds(start, GROUP)]

            center = plane(0)
            sums = [center * float((radius + 1) ** 2) for radius in RADII]
            for k in range(1, R_LARGE + 1):
                pair = plane(-k) + plane(k)
                for f, radius in enumerate(RADII):
                    if k <= radius:
                        sums[f] = sums[f] + pair * float((radius + 1) ** 2 - k * k)
            for f in range(2):
                high, low = split(sums[f])
                xb[f, i, pl.ds(base, GROUP)] = high
                xb[f, i, pl.ds(rows + base, GROUP)] = low
            return carry

        lax.fori_loop(0, nx, one, 0, unroll=4)

    slots = lax.div(iota((STRIP, nz), 1), H)

    def smooth_y(u, keep=True, send=True):
        base = (u % strips) * STRIP
        for f in range(2):
            up = jnp.zeros((STRIP, nz), F32)
            down = jnp.zeros((STRIP, nz), F32)
            for p in range(0, nx, 2):
                both = jnp.concatenate(
                    [jnp.concatenate([xb[f, p + j, pl.ds(base, wide)],
                                      xb[f, p + j, pl.ds(rows + base, wide)]], axis=0)
                     for j in range(2)], axis=1)
                done = jnp.dot(wy[f], both, preferred_element_type=F32)
                for j in range(2):
                    value = done[:, j * nz:(j + 1) * nz]
                    if send:
                        rolled = pltpu.roll(value, ((p + j + 1) * H) % nz, 1)
                        up = jnp.where(slots == p + j, rolled, up)
                        down = jnp.where(slots == (p + j + 1) % nx, rolled, down)
                    if keep:
                        high, low = split(value)
                        zb[f, p + j, :, pl.ds(0, nz)] = high
                        zb[f, p + j, :, pl.ds(nz, nz)] = low
            if send:
                zsend[u, 0, pl.ds(f * STRIP, STRIP)] = up
                zsend[u, 1, pl.ds(f * STRIP, STRIP)] = down
        if send:
            for d in range(2):
                z_copy(u, d).start()

    def main_z(u):
        slot = u % 2
        for f in range(2):
            for p in range(0, nx, 8):
                block = zb[f, pl.ds(p, 8)].reshape(8 * STRIP, 2 * nz)
                done = jnp.dot(block, wm[f], preferred_element_type=F32)
                zm[slot, f, pl.ds(p, 8)] = done.reshape(8, STRIP, nz)

    def finish(u):
        slot = u % 2
        s, h = divmod(u, strips)
        part = pl.ds(h * STRIP, STRIP)
        for d in range(2):
            z_copy(u, d).wait_recv()
        halves = []
        for f in range(2):
            own = pl.ds(f * STRIP, STRIP)
            packed = jnp.concatenate([zrecv[u, 0, own], zrecv[u, 1, own]], axis=1)
            halves.append(jnp.concatenate(split(packed), axis=0))
        for p in range(0, nx, 2):
            level = []
            for f, (radius, less) in enumerate(zip(RADII, (0.3, 0.1))):
                done = jnp.dot(halves[f], wh[f, p // 2], preferred_element_type=F32)
                done = done[:STRIP] + done[STRIP:]
                pair = []
                for j in range(2):
                    smooth = (zm[slot, f, p + j] + done[:, j * nz:(j + 1) * nz]) * scale_of(radius)
                    pair.append(effv[p + j, part] * smooth - less)
                level.append(pair)
            for j in range(2):
                top = jnp.maximum(level[0][j], level[1][j])
                outv[s, p + j, part] = jnp.clip(0.5 + 0.25 * top, 0.0, 1.0)

    units = snaps * strips

    def outer_lanes_ahead():
        for d in range(2):
            t_copy(d).wait_recv()
            packed = trecv[d]
            for p in range(H):
                near_x[(0 if d == 0 else nx + H) + p] = pltpu.roll(
                    packed, nz - p * 2 * H - H, 1)
        for p in range(nx):
            near_x[H + p] = ext[final, H + p, last_rows]
        smooth_x(near_x, 0, last)
        smooth_y(units - 1, keep=False)

    for s in range(snaps):
        if s != final:
            own_copy(s).wait()
        for d in range(2):
            y_copy(s, d).wait_recv()
            for q in range(2):
                f_copy(s, q, d).wait_recv()
        for g in edge:
            smooth_x(ext.at[s], g * GROUP, g)
        held = set(edge)
        done = 0
        for together in arrivals(s):
            for d in range(2):
                x_copy(s, together, d).wait_recv()
            for g in together:
                smooth_x(ext.at[s], g * GROUP, g)
            held.update(together)
            if s == final and held == set(range(first_needed, groups)) - {last} | set(edge):
                outer_lanes_ahead()
            while done < strips and held.issuperset(
                    range(done * STRIP // GROUP, (done * STRIP + wide) // GROUP)):
                u = s * strips + done
                smooth_y(u, send=u != units - 1)
                main_z(u)
                if u == 0:
                    eff_copy.wait()
                else:
                    finish(u - 1)
                done += 1
    finish(units - 1)

    for s in range(snaps):
        for d in range(2):
            for together in tuple((g,) for g in edge) + arrivals(s):
                x_copy(s, together, d).wait_send()
            y_copy(s, d).wait_send()
            for q in range(2):
                f_copy(s, q, d).wait_send()
    for d in range(2):
        t_copy(d).wait_send()
    for u in range(units):
        for d in range(2):
            z_copy(u, d).wait_send()


def on_device(density, efficiency):
    snaps, nx, ny, nz = density.shape
    rows = ny + 2 * H
    groups = rows // GROUP
    units = snaps * (ny // STRIP)
    dma = pltpu.SemaphoreType.DMA
    return pl.pallas_call(
        kernel,
        out_shape=pltpu.VMEM(density.shape, F32),
        in_specs=[pl.BlockSpec(memory_space=pl.ANY)] * 2,
        out_specs=pl.BlockSpec(memory_space=pltpu.VMEM),
        scratch_shapes=[
            pltpu.VMEM((snaps, nx + 2 * H, rows, nz), F32),
            pltpu.VMEM((nx, ny, nz), F32),
            pltpu.VMEM((2, nx, 2 * rows, nz), BF16),
            pltpu.VMEM((2, nx, STRIP, 2 * nz), BF16),
            pltpu.VMEM((2, 2, nx, STRIP, nz), F32),
            pltpu.VMEM((units, 2, 2 * STRIP, nx * H), F32),
            pltpu.VMEM((units, 2, 2 * STRIP, nx * H), F32),
            pltpu.VMEM((2, STRIP, 2 * (STRIP + 2 * H)), BF16),
            pltpu.VMEM((2, 2 * nz, nz), BF16),
            pltpu.VMEM((2, nx // 2, 2 * nx * H, 2 * nz), BF16),
            pltpu.VMEM((nx + 2 * H, GROUP, nz), F32),
            pltpu.VMEM((2, GROUP, nz), F32),
            pltpu.VMEM((2, GROUP, nz), F32),
            dma((snaps, groups, 2)), dma((snaps, groups, 2)),
            dma((snaps, 2)), dma((snaps, 2)),
            dma((snaps, 2, 2)), dma((snaps, 2, 2)),
            dma((units, 2)), dma((units, 2)),
            dma((2,)), dma((2,)),
            dma((snaps,)), dma,
        ],
        compiler_params=pltpu.CompilerParams(
            collective_id=0, has_side_effects=True),
    )(density, efficiency)


def solution(mesh):
    placed = (P(None, "gx", "gy", "gz"), P("gx", "gy", "gz"))
    return jax.shard_map(
        on_device, mesh=mesh, in_specs=placed, out_specs=P(None, "gx", "gy", "gz"), check_vma=False
    )
```

```python
import functools
import math

import jax
import jax.numpy as jnp
from jax import lax
from jax.experimental import pallas as pl
from jax.experimental.pallas import tpu as pltpu
from jax.sharding import PartitionSpec as P

R_SMALL = 4
R_LARGE = 8
RADII = (R_SMALL, R_LARGE)
H = R_LARGE
GROUP = 16
STRIP = 32
F32 = jnp.float32
BF16 = jnp.bfloat16
MESH = pl.DeviceIdType.MESH


def scale_of(radius):
    raw = [(radius + 1) ** 2 - k * k for k in range(-radius, radius + 1)]
    return 1.0 / math.sqrt(sum(value * value for value in raw)) ** 3


def band(offset, radius):
    value = (radius + 1) ** 2 - offset * offset
    return jnp.where(jnp.abs(offset) <= radius, value, 0).astype(F32).astype(BF16)


def split(value):
    high = value.astype(BF16)
    return high, (value - high.astype(F32)).astype(BF16)


def iota(shape, dim):
    return lax.broadcasted_iota(jnp.int32, shape, dim)


def kernel(dens, eff, outv, ext, effv, xb, zb, zm, zsend, zrecv, wy, wm, wh, near_x, tsend, trecv,
           x_send, x_recv, y_send, y_recv, f_send, f_recv, z_send, z_recv, t_send, t_recv,
           own_sem, eff_sem):
    snaps, nx, ny, nz = dens.shape
    rows = ny + 2 * H
    groups = rows // GROUP
    strips = ny // STRIP
    wide = STRIP + 2 * H
    near = {}
    for axis in ("gx", "gy", "gz"):
        count = lax.axis_size(axis)
        me = lax.axis_index(axis)
        near[axis] = (lax.rem(me + 1, count), lax.rem(me + count - 1, count))

    def own_copy(s):
        return pltpu.make_async_copy(
            dens.at[s], ext.at[s, pl.ds(H, nx), pl.ds(H, ny)], own_sem.at[s])

    eff_copy = pltpu.make_async_copy(eff, effv, eff_sem)

    final = snaps - 1
    edge = (0, groups - 1)
    inner = tuple(range(1, groups - 1))
    last = inner[-1]
    first_needed = (strips - 1) * STRIP // GROUP
    ordered = tuple(sorted(inner, key=lambda g: (g == last, g < first_needed)))

    def arrivals(s):
        return tuple((g,) for g in ordered) if s == final else (inner,)

    def x_copy(s, together, d):
        start = max(together[0] * GROUP - H, 0)
        size = min((together[-1] + 1) * GROUP - H, ny) - start
        source = nx - H if d == 0 else 0
        target = 0 if d == 0 else nx + H
        g = together[0]
        return pltpu.make_async_remote_copy(
            src_ref=dens.at[s, pl.ds(source, H), pl.ds(start, size)],
            dst_ref=ext.at[s, pl.ds(target, H), pl.ds(H + start, size)],
            send_sem=x_send.at[s, g, d], recv_sem=x_recv.at[s, g, d],
            device_id={"gx": near["gx"][d]}, device_id_type=MESH)

    def t_copy(d):
        return pltpu.make_async_remote_copy(
            src_ref=tsend.at[d], dst_ref=trecv.at[d],
            send_sem=t_send.at[d], recv_sem=t_recv.at[d],
            device_id={"gx": near["gx"][d]}, device_id_type=MESH)

    def y_copy(s, d):
        source = ny - H if d == 0 else 0
        target = 0 if d == 0 else ny + H
        return pltpu.make_async_remote_copy(
            src_ref=dens.at[s, :, pl.ds(source, H)],
            dst_ref=ext.at[s, pl.ds(H, nx), pl.ds(target, H)],
            send_sem=y_send.at[s, d], recv_sem=y_recv.at[s, d],
            device_id={"gy": near["gy"][d]}, device_id_type=MESH)

    def f_copy(s, q, d):
        planes = 0 if q == 0 else nx + H
        source = ny if d == 0 else H
        target = 0 if d == 0 else ny + H
        return pltpu.make_async_remote_copy(
            src_ref=ext.at[s, pl.ds(planes, H), pl.ds(source, H)],
            dst_ref=ext.at[s, pl.ds(planes, H), pl.ds(target, H)],
            send_sem=f_send.at[s, q, d], recv_sem=f_recv.at[s, q, d],
            device_id={"gy": near["gy"][d]}, device_id_type=MESH)

    def z_copy(u, d):
        return pltpu.make_async_remote_copy(
            src_ref=zsend.at[u, d], dst_ref=zrecv.at[u, d],
            send_sem=z_send.at[u, d], recv_sem=z_recv.at[u, d],
            device_id={"gz": near["gz"][d]}, device_id_type=MESH)

    for s in range(snaps):
        own_copy(s).start()
    eff_copy.start()

    barrier = pltpu.get_barrier_semaphore()
    for axis in ("gx", "gy", "gz"):
        for d in range(2):
            pl.semaphore_signal(
                barrier, inc=1, device_id={axis: near[axis][d]}, device_id_type=MESH)
    pl.semaphore_wait(barrier, 6)

    at_top = lax.axis_index("gx") == lax.axis_size("gx") - 1

    def start_pieces(pieces, first):
        for piece in pieces:
            x_copy(*piece, first).start()
            x_copy(*piece, 1 - first).start()

    def send_x(pieces):
        @pl.when(at_top)
        def _():
            start_pieces(pieces, 0)

        @pl.when(jnp.logical_not(at_top))
        def _():
            start_pieces(pieces, 1)

    send_x([(s, (g,)) for s in range(snaps) for g in edge])
    for s in range(snaps):
        for d in range(2):
            y_copy(s, d).start()

    own_copy(final).wait()
    last_rows = pl.ds(last * GROUP, GROUP)
    pieces = lax.div(iota((GROUP, nz), 1), 2 * H)
    for d in range(2):
        packed = jnp.zeros((GROUP, nz), F32)
        for p in range(H):
            plane = ext[final, (nx if d == 0 else H) + p, last_rows]
            packed = jnp.where(pieces == p, pltpu.roll(plane, p * 2 * H + H, 1), packed)
        tsend[d] = packed
        t_copy(d).start()

    send_x([(s, together) for s in range(snaps) for together in arrivals(s)])

    for f, radius in enumerate(RADII):
        shape = (STRIP, wide)
        along = band(iota(shape, 1) - iota(shape, 0) - H, radius)
        wy[f] = jnp.concatenate([along, along], axis=1)
        shape = (nz, nz)
        along = band(iota(shape, 1) - iota(shape, 0), radius)
        wm[f] = jnp.concatenate([along, along], axis=0)
        shape = (nx * H, nz)
        slot = lax.div(iota(shape, 0), H)
        cell = lax.rem(iota(shape, 0), H)
        lane = iota(shape, 1)
        low = band(cell - H - lane, radius)
        high = band(cell + nz - lane, radius)
        zero = jnp.zeros_like(low)
        for p in range(nx):
            low_p = jnp.where(slot == p, low, zero)
            high_p = jnp.where(slot == (p + 1) % nx, high, zero)
            wh[f, p // 2, pl.ds(0, nx * H), pl.ds((p % 2) * nz, nz)] = low_p
            wh[f, p // 2, pl.ds(nx * H, nx * H), pl.ds((p % 2) * nz, nz)] = high_p

    for s in range(snaps):
        for d, g in ((0, groups - 1), (1, 0)):
            for q in range(2):
                x_copy(s, (g,), q).wait_recv()
                f_copy(s, q, d).start()

    def smooth_x(field, start, g):
        base = g * GROUP

        def one(i, carry):
            def plane(k):
                return field[i + (H + k), pl.ds(start, GROUP)]

            center = plane(0)
            sums = [center * float((radius + 1) ** 2) for radius in RADII]
            for k in range(1, R_LARGE + 1):
                pair = plane(-k) + plane(k)
                for f, radius in enumerate(RADII):
                    if k <= radius:
                        sums[f] = sums[f] + pair * float((radius + 1) ** 2 - k * k)
            for f in range(2):
                high, low = split(sums[f])
                xb[f, i, pl.ds(base, GROUP)] = high
                xb[f, i, pl.ds(rows + base, GROUP)] = low
            return carry

        lax.fori_loop(0, nx, one, 0, unroll=16)

    slots = lax.div(iota((STRIP, nz), 1), H)

    def smooth_y(u, keep=True, send=True):
        base = (u % strips) * STRIP
        for f in range(2):
            up = jnp.zeros((STRIP, nz), F32)
            down = jnp.zeros((STRIP, nz), F32)
            for p in range(0, nx, 2):
                both = jnp.concatenate(
                    [jnp.concatenate([xb[f, p + j, pl.ds(base, wide)],
                                      xb[f, p + j, pl.ds(rows + base, wide)]], axis=0)
                     for j in range(2)], axis=1)
                done = jnp.dot(wy[f], both, preferred_element_type=F32)
                for j in range(2):
                    value = done[:, j * nz:(j + 1) * nz]
                    if send:
                        rolled = pltpu.roll(value, ((p + j + 1) * H) % nz, 1)
                        up = jnp.where(slots == p + j, rolled, up)
                        down = jnp.where(slots == (p + j + 1) % nx, rolled, down)
                    if keep:
                        high, low = split(value)
                        zb[f, p + j, :, pl.ds(0, nz)] = high
                        zb[f, p + j, :, pl.ds(nz, nz)] = low
            if send:
                zsend[u, 0, pl.ds(f * STRIP, STRIP)] = up
                zsend[u, 1, pl.ds(f * STRIP, STRIP)] = down
        if send:
            for d in range(2):
                z_copy(u, d).start()

    def main_z(u):
        slot = u % 2
        for f in range(2):
            for p in range(0, nx, 8):
                block = zb[f, pl.ds(p, 8)].reshape(8 * STRIP, 2 * nz)
                done = jnp.dot(block, wm[f], preferred_element_type=F32)
                zm[slot, f, pl.ds(p, 8)] = done.reshape(8, STRIP, nz)

    def finish(u):
        slot = u % 2
        s, h = divmod(u, strips)
        part = pl.ds(h * STRIP, STRIP)
        for d in range(2):
            z_copy(u, d).wait_recv()
        halves = []
        for f in range(2):
            own = pl.ds(f * STRIP, STRIP)
            packed = jnp.concatenate([zrecv[u, 0, own], zrecv[u, 1, own]], axis=1)
            halves.append(jnp.concatenate(split(packed), axis=0))
        for p in range(0, nx, 2):
            level = []
            for f, (radius, less) in enumerate(zip(RADII, (0.3, 0.1))):
                done = jnp.dot(halves[f], wh[f, p // 2], preferred_element_type=F32)
                done = done[:STRIP] + done[STRIP:]
                pair = []
                for j in range(2):
                    smooth = (zm[slot, f, p + j] + done[:, j * nz:(j + 1) * nz]) * scale_of(radius)
                    pair.append(effv[p + j, part] * smooth - less)
                level.append(pair)
            for j in range(2):
                top = jnp.maximum(level[0][j], level[1][j])
                outv[s, p + j, part] = jnp.clip(0.5 + 0.25 * top, 0.0, 1.0)

    units = snaps * strips

    def outer_lanes_ahead():
        for d in range(2):
            t_copy(d).wait_recv()
            packed = trecv[d]
            for p in range(H):
                near_x[(0 if d == 0 else nx + H) + p] = pltpu.roll(
                    packed, nz - p * 2 * H - H, 1)
        for p in range(nx):
            near_x[H + p] = ext[final, H + p, last_rows]
        smooth_x(near_x, 0, last)
        smooth_y(units - 1, keep=False)

    for s in range(snaps):
        if s != final:
            own_copy(s).wait()
        for d in range(2):
            y_copy(s, d).wait_recv()
            for q in range(2):
                f_copy(s, q, d).wait_recv()
        for g in edge:
            smooth_x(ext.at[s], g * GROUP, g)
        held = set(edge)
        done = 0
        for together in arrivals(s):
            for d in range(2):
                x_copy(s, together, d).wait_recv()
            for g in together:
                smooth_x(ext.at[s], g * GROUP, g)
            held.update(together)
            if s == final and held == set(range(first_needed, groups)) - {last} | set(edge):
                outer_lanes_ahead()
            while done < strips and held.issuperset(
                    range(done * STRIP // GROUP, (done * STRIP + wide) // GROUP)):
                u = s * strips + done
                smooth_y(u, send=u != units - 1)
                main_z(u)
                if u == 0:
                    eff_copy.wait()
                else:
                    finish(u - 1)
                done += 1
    finish(units - 1)

    for s in range(snaps):
        for d in range(2):
            for together in tuple((g,) for g in edge) + arrivals(s):
                x_copy(s, together, d).wait_send()
            y_copy(s, d).wait_send()
            for q in range(2):
                f_copy(s, q, d).wait_send()
    for d in range(2):
        t_copy(d).wait_send()
    for u in range(units):
        for d in range(2):
            z_copy(u, d).wait_send()


def on_device(density, efficiency):
    snaps, nx, ny, nz = density.shape
    rows = ny + 2 * H
    groups = rows // GROUP
    units = snaps * (ny // STRIP)
    dma = pltpu.SemaphoreType.DMA
    return pl.pallas_call(
        kernel,
        out_shape=pltpu.VMEM(density.shape, F32),
        in_specs=[pl.BlockSpec(memory_space=pl.ANY)] * 2,
        out_specs=pl.BlockSpec(memory_space=pltpu.VMEM),
        scratch_shapes=[
            pltpu.VMEM((snaps, nx + 2 * H, rows, nz), F32),
            pltpu.VMEM((nx, ny, nz), F32),
            pltpu.VMEM((2, nx, 2 * rows, nz), BF16),
            pltpu.VMEM((2, nx, STRIP, 2 * nz), BF16),
            pltpu.VMEM((2, 2, nx, STRIP, nz), F32),
            pltpu.VMEM((units, 2, 2 * STRIP, nx * H), F32),
            pltpu.VMEM((units, 2, 2 * STRIP, nx * H), F32),
            pltpu.VMEM((2, STRIP, 2 * (STRIP + 2 * H)), BF16),
            pltpu.VMEM((2, 2 * nz, nz), BF16),
            pltpu.VMEM((2, nx // 2, 2 * nx * H, 2 * nz), BF16),
            pltpu.VMEM((nx + 2 * H, GROUP, nz), F32),
            pltpu.VMEM((2, GROUP, nz), F32),
            pltpu.VMEM((2, GROUP, nz), F32),
            dma((snaps, groups, 2)), dma((snaps, groups, 2)),
            dma((snaps, 2)), dma((snaps, 2)),
            dma((snaps, 2, 2)), dma((snaps, 2, 2)),
            dma((units, 2)), dma((units, 2)),
            dma((2,)), dma((2,)),
            dma((snaps,)), dma,
        ],
        compiler_params=pltpu.CompilerParams(
            collective_id=0, has_side_effects=True),
    )(density, efficiency)


def solution(mesh):
    placed = (P(None, "gx", "gy", "gz"), P("gx", "gy", "gz"))
    return jax.shard_map(
        on_device, mesh=mesh, in_specs=placed, out_specs=P(None, "gx", "gy", "gz"), check_vma=False
    )
```
